256 devices in a mesh: seg: 8 (over y, core), chan: 32 (over z, x).
Axes of the slice: x: 4, y: 4, z: 8, core: 2. Of those that a mesh axis runs over, the one named last changes fastest.
Arguments:
- spectra: bfloat16 [8, 8192, 2, 2048], P('seg', 'chan'), may hold values from -40 to 40
- source_ids: int32 [64], replicated, may hold values from 0 to 8191, as said below
- pair_source: int32 [32768], P('chan'), may hold values from 0 to 63
- pair_offset: int32 [32768], P('chan'), may hold values from -128 to 383, as said below
- pair_counts: int32 [32], P('chan'), may hold values from 256 to 1024, as said below
Outputs:
- correlations: float32 [1024, 32768], P('seg', 'chan')
The draws below stay inside these ranges and needn't reach their ends.
Inputs may be any that keep to these rules, and one draw needn't show every extreme that they name: `source_ids`: distinct channels. `pair_offset`: blocks at the fibre's ends never reach beyond it: block 0 has offsets of 0 or more, the last block offsets under 256. `pair_counts`: one block holds exactly 1024 live slots in every draw; the others hold 256 to 768.
All inputs are finite; a program needn't handle non-finite values.
Results may differ from the reference program's by a relative error of at most 0.0055.
Values may be sent and summed in bfloat16 or wider, within the bound.
A program may use at most 192 MiB of HBM per device.

```python
import math
import jax
import jax.numpy as jnp
from jax import lax

FREQ = 2048
SOURCES = 64
LAGS = 1024
WBLOCK = 64
CH_DEV = 256
PAIR_CAP = 1024
SEGS = 8
CHANNELS = 8192
BAND = 128
PAIRS_ALL = 32768
N_CHAN = 32


def draw_spectra(key, part):
    key_base = jax.random.fold_in(key, 11)
    key_chan = jax.random.fold_in(key, 12)
    key_bins = jax.random.fold_in(key, 13)
    key_segs = jax.random.fold_in(key, 14)
    base = jnp.clip(jax.random.normal(key_base, (SEGS, CHANNELS, 2, FREQ), jnp.float32), -4.0, 4.0)
    low, high = (math.log(0.3), math.log(3.0))
    chan_gain = jnp.exp(jax.random.uniform(key_chan, (1, CHANNELS, 1, 1), jnp.float32, low, high))
    bin_gain = jnp.exp(jax.random.uniform(key_bins, (1, 1, 1, FREQ), jnp.float32, low, high))
    seg_gain = jnp.exp(jax.random.uniform(key_segs, (SEGS, 1, 1, 1), jnp.float32, -0.5, 0.5))
    return jnp.clip(base * chan_gain * bin_gain * seg_gain, -40.0, 40.0).astype(jnp.bfloat16)


def draw_source_ids(key, part):
    order = jax.random.permutation(jax.random.fold_in(key, 21), CHANNELS)
    return order[:SOURCES].astype(jnp.int32)


def draw_pair_offset(key, part):
    block_total = PAIRS_ALL // PAIR_CAP
    block_index = jnp.arange(block_total, dtype=jnp.int32)[:, None]
    lower = jnp.where(block_index == 0, 0, -BAND).astype(jnp.int32)
    upper = jnp.where(block_index == block_total - 1, CH_DEV, CH_DEV + BAND).astype(jnp.int32)
    lower = jnp.broadcast_to(lower, (block_total, PAIR_CAP))
    upper = jnp.broadcast_to(upper, (block_total, PAIR_CAP))
    picked = jax.random.randint(jax.random.fold_in(key, 31), (block_total, PAIR_CAP), lower, upper, jnp.int32)
    return picked.reshape(PAIRS_ALL)


def draw_pair_counts(key, part):
    block_total = PAIRS_ALL // PAIR_CAP
    counts = jax.random.randint(jax.random.fold_in(key, 41), (block_total,), PAIR_CAP // 4, 3 * PAIR_CAP // 4 + 1, jnp.int32)
    busiest = jax.random.randint(jax.random.fold_in(key, 42), (), 0, block_total, jnp.int32)
    filled = jnp.arange(block_total, dtype=jnp.int32) == busiest
    return jnp.where(filled, PAIR_CAP, counts).astype(jnp.int32)


def plant(entries, rng, smallest, largest):
    extent = entries.shape
    spot = [jax.random.randint(jax.random.fold_in(rng, axis), (), 0, extent[axis]) for axis in range(len(extent))]
    entries = entries.at[tuple(spot)].set(smallest)
    longest = extent.index(max(extent))
    spot[longest] = (spot[longest] + 1) % extent[longest]
    return entries.at[tuple(spot)].set(largest)


def setup_inputs(seed: int = 0) -> dict:
    keys = jax.random.split(jax.random.key(seed), 6)
    spectra = draw_spectra(jax.random.fold_in(keys[5], 71), 0)
    source_ids = draw_source_ids(jax.random.fold_in(keys[5], 71), 0)
    pair_source = plant(jax.random.randint(keys[2], (PAIRS_ALL,), 0, SOURCES), jax.random.fold_in(keys[2], 1), 0, SOURCES - 1).astype(jnp.int32)
    pair_offset = draw_pair_offset(jax.random.fold_in(keys[5], 71), 0)
    pair_counts = draw_pair_counts(jax.random.fold_in(keys[5], 71), 0)
    return dict(spectra=spectra, source_ids=source_ids, pair_source=pair_source, pair_offset=pair_offset, pair_counts=pair_counts)


def whiten(values):
    power = values[..., 0, :] ** 2 + values[..., 1, :] ** 2
    grouped = power.reshape(power.shape[:-1] + (FREQ // WBLOCK, WBLOCK))
    level = lax.optimization_barrier(jnp.mean(grouped, axis=-1))
    inverse = lax.rsqrt(level + 1e-06)
    spread = jnp.repeat(inverse, WBLOCK, axis=-1)
    return (values * spread[..., None, :]).astype(jnp.bfloat16)

def lag_matrix(start, count, total_segs):
    lag_steps = start + jnp.arange(count, dtype=jnp.int32) - LAGS // 2
    bin_steps = jnp.arange(FREQ, dtype=jnp.int32)
    phase = jnp.mod(lag_steps[:, None] * bin_steps[None, :], 2 * FREQ).astype(jnp.float32)
    theta = phase * (math.pi / FREQ)
    factor = 1.0 / math.sqrt(FREQ * total_segs)
    return jnp.concatenate([jnp.cos(theta) * factor, -jnp.sin(theta) * factor], axis=1).astype(jnp.bfloat16)

def cross_spectrum(source_rows, receiver_rows, live_slots):
    src_f = source_rows.astype(jnp.float32)
    rec_f = receiver_rows.astype(jnp.float32)
    real_part = src_f[:, 0] * rec_f[:, 0] + src_f[:, 1] * rec_f[:, 1]
    imag_part = src_f[:, 1] * rec_f[:, 0] - src_f[:, 0] * rec_f[:, 1]
    joined = jnp.concatenate([real_part, imag_part], axis=1).astype(jnp.bfloat16)
    return jnp.where(live_slots[:, None], joined, jnp.zeros_like(joined))

def reference(spectra, source_ids, pair_source, pair_offset, pair_counts):
    whitened = lax.map(lambda segment: whiten(segment.astype(jnp.float32)), spectra)
    source_spec = whitened[:, source_ids]
    lag_table = lag_matrix(0, LAGS, SEGS).astype(jnp.float32)
    blocks_src = pair_source.reshape(N_CHAN, PAIR_CAP)
    blocks_off = pair_offset.reshape(N_CHAN, PAIR_CAP)

    def one_block(packed):
        block_index, block_src, block_off, block_count = packed
        receivers = block_index * CH_DEV + block_off
        live_slots = jnp.arange(PAIR_CAP, dtype=jnp.int32) < block_count
        stacked = jnp.zeros((PAIR_CAP, 2 * FREQ), jnp.float32)
        for segment in range(SEGS):
            cross_spec = cross_spectrum(source_spec[segment][block_src], whitened[segment][receivers], live_slots)
            stacked = stacked + cross_spec.astype(jnp.float32)
        return jnp.dot(lag_table, stacked.T, precision=lax.Precision.HIGHEST, preferred_element_type=jnp.float32)
    results = lax.map(one_block, (jnp.arange(N_CHAN, dtype=jnp.int32), blocks_src, blocks_off, pair_counts))
    return jnp.transpose(results, (1, 0, 2)).reshape(LAGS, N_CHAN * PAIR_CAP)
```

```python
import functools
import math

import jax
import jax.numpy as jnp
import ml_dtypes
import numpy as np
from jax import lax
from jax.experimental import pallas as pl
from jax.experimental.pallas import tpu as pltpu
from jax.sharding import PartitionSpec as P

MESH = pl.DeviceIdType.MESH
WBLOCK = 64
BINS = 256
TILE = 256
CORES = 2
NX = 4


def lag_table(lags, freq, segs):
    tau = np.arange(lags, dtype=np.int64)[:, None] - lags // 2
    phase = np.mod(tau * np.arange(freq, dtype=np.int64)[None, :], 2 * freq)
    theta = phase * (math.pi / freq)
    scale = 1.0 / math.sqrt(freq * segs)
    both = np.stack([np.cos(theta) * scale, -np.sin(theta) * scale])
    both = both.astype(np.float32).astype(ml_dtypes.bfloat16)
    chunks = freq // BINS
    both = both.reshape(2, lags, chunks, BINS).transpose(2, 1, 0, 3)
    return both.reshape(chunks, lags, 2 * BINS)


def dot(a, b):
    return jnp.dot(a, b, preferred_element_type=jnp.float32)


def kernel(
    nz, ny, ids_ref, psrc_ref, poff_ref, cnt_ref, raw_ref, tab_hbm, out_ref,
    tab, rows, pick, slab_in, slab, part_in, srcs, src_t, hot_r, hot_s, acc,
    core_out, core_in, y_out, y_in, y_own,
    tab_sem, halo_send, halo_recv, x1_send, x1_recv, z1_send, z1_recv,
    z2_send, z2_recv, x2_send, x2_recv, core_send, core_recv, y_send, y_recv,
):
    chunks, _, chans, _ = raw_ref.shape
    band = chans // 2
    slots = psrc_ref.shape[1]
    n_src = pick.shape[1]
    tiles = slots // TILE
    out_rows = out_ref.shape[0]
    per = pick.shape[0] // (NX * nz)
    seg, chan = lax.axis_index("seg"), lax.axis_index("chan")
    n_chan = NX * nz
    my, mc = seg // CORES, seg % CORES
    mz, mx = chan // NX, chan % NX
    left, right = (chan + n_chan - 1) % n_chan, (chan + 1) % n_chan
    other = my * CORES + (1 - mc)

    def x_peer(d):
        return mz * NX + (mx + d) % NX

    def z_peer(d):
        return ((mz + d) % nz) * NX + mx

    def y_peer(d):
        return ((my + d) % ny) * CORES + mc

    def remote(src, dst, send, recv, **where):
        return pltpu.make_async_remote_copy(
            src_ref=src, dst_ref=dst, send_sem=send, recv_sem=recv,
            device_id=where, device_id_type=MESH,
        )

    for f in range(chunks):
        pltpu.make_async_copy(tab_hbm.at[f], tab.at[f], tab_sem.at[f]).start()

    barrier = pltpu.get_barrier_semaphore()
    met = 0
    for peer in [left, right] + [x_peer(d) for d in range(1, NX)] + [z_peer(d) for d in range(1, nz)]:
        pl.semaphore_signal(barrier, inc=1, device_id={"chan": peer}, device_id_type=MESH)
        met += 1
    for peer in [other] + [y_peer(d) for d in range(1, ny)]:
        pl.semaphore_signal(barrier, inc=1, device_id={"seg": peer}, device_id_type=MESH)
        met += 1
    pl.semaphore_wait(barrier, met)

    def halo_left(f):
        return remote(
            rows.at[f, :, pl.ds(band, band)], rows.at[f, :, pl.ds(band + chans, band)],
            halo_send.at[0, f], halo_recv.at[0, f], chan=left,
        )

    def halo_right(f):
        return remote(
            rows.at[f, :, pl.ds(2 * band, band)], rows.at[f, :, pl.ds(0, band)],
            halo_send.at[1, f], halo_recv.at[1, f], chan=right,
        )

    lane = lax.broadcasted_iota(jnp.int32, (BINS, BINS), 1)
    sub = lax.broadcasted_iota(jnp.int32, (BINS, BINS), 0)
    mean_of = jnp.where(lane // WBLOCK == sub // WBLOCK, 1.0 / WBLOCK, 0.0).astype(jnp.bfloat16)
    local = ids_ref[...] - chan * chans
    sel_t = jnp.where(
        lax.broadcasted_iota(jnp.int32, (chans, local.shape[1]), 0) == local, 1.0, 0.0
    )
    sel = jnp.transpose(sel_t)[:n_src].astype(jnp.bfloat16)

    def whiten(f, carry):
        re = raw_ref[f, 0].astype(jnp.float32)
        im = raw_ref[f, 1].astype(jnp.float32)
        power = re * re + im * im
        hi = power.astype(jnp.bfloat16)
        rest = power - hi.astype(jnp.float32)
        mid = rest.astype(jnp.bfloat16)
        low = (rest - mid.astype(jnp.float32)).astype(jnp.bfloat16)
        level = dot(hi, mean_of) + (dot(mid, mean_of) + dot(low, mean_of))
        inverse = lax.rsqrt(level + 1e-06)
        for p, val in enumerate((re, im)):
            white = (val * inverse).astype(jnp.bfloat16)
            got = dot(sel, white).astype(jnp.bfloat16)
            for h in range(2):
                pick[f * 4 + p * 2 + h] = got[:, h * 128:(h + 1) * 128]
            rows[f, pl.ds(p * BINS, BINS), pl.ds(band, chans)] = jnp.transpose(white)
        halo_left(f).start()
        halo_right(f).start()
        return carry

    lax.fori_loop(0, chunks, whiten, 0)

    step = per * nz

    def x1(d):
        return remote(
            pick.at[pl.ds(((mx + d) % NX) * step, step)], slab_in.at[d - 1],
            x1_send.at[d - 1], x1_recv.at[d - 1], chan=x_peer(d),
        )

    def z1(d):
        return remote(
            slab.at[pl.ds(((mz + d) % nz) * per, per)], part_in.at[d - 1],
            z1_send.at[d - 1], z1_recv.at[d - 1], chan=z_peer(d),
        )

    mine = mx * step + mz * per

    def z2(d):
        return remote(
            srcs.at[pl.ds(mine, per)], srcs.at[pl.ds(mine, per)],
            z2_send.at[d - 1], z2_recv.at[d - 1], chan=z_peer(d),
        )

    def x2(d):
        return remote(
            srcs.at[pl.ds(mx * step, step)], srcs.at[pl.ds(mx * step, step)],
            x2_send.at[d - 1], x2_recv.at[d - 1], chan=x_peer(d),
        )

    for d in range(1, NX):
        x1(d).start()

    at = poff_ref[...] + band
    src_at = psrc_ref[...]
    live = lax.broadcasted_iota(jnp.int32, (1, slots), 1) < cnt_ref[...]
    src_at = jnp.where(live, src_at, -1)
    for t in range(tiles):
        cut = slice(t * TILE, (t + 1) * TILE)
        hot_r[t] = jnp.where(
            lax.broadcasted_iota(jnp.int32, (2 * chans, TILE), 0) == at[:, cut], 1.0, 0.0
        ).astype(jnp.bfloat16)
        hot_s[t] = jnp.where(
            lax.broadcasted_iota(jnp.int32, (n_src, TILE), 0) == src_at[:, cut], 1.0, 0.0
        ).astype(jnp.bfloat16)

    for d in range(1, NX):
        x1(d).wait_recv()
    total = pick[pl.ds(mx * step, step)]
    for d in range(1, NX):
        total = total + slab_in[d - 1]
    slab[...] = total
    for d in range(1, nz):
        z1(d).start()
    for d in range(1, nz):
        z1(d).wait_recv()
    total = slab[pl.ds(mz * per, per)]
    for d in range(1, nz):
        total = total + part_in[d - 1]
    srcs[pl.ds(mine, per)] = total
    for d in range(1, nz):
        z2(d).start()
    for d in range(1, nz):
        z2(d).wait_recv()
    for d in range(1, NX):
        x2(d).start()
    for d in range(1, NX):
        x2(d).wait_recv()

    def turn(f, carry):
        for p in range(2):
            both = jnp.concatenate([srcs[f * 4 + p * 2], srcs[f * 4 + p * 2 + 1]], axis=1)
            src_t[f, pl.ds(p * BINS, BINS), :] = jnp.transpose(both)
        return carry

    lax.fori_loop(0, chunks, turn, 0)

    def piece(f, t):
        rec = dot(rows[f], hot_r[t])
        src = dot(src_t[f], hot_s[t])
        rr, ri, sr, si = rec[:BINS], rec[BINS:], src[:BINS], src[BINS:]
        cross = jnp.concatenate([sr * rr + si * ri, si * rr - sr * ri], axis=0)
        return dot(tab[f], cross.astype(jnp.bfloat16))

    def chunk_step(f, carry):
        pltpu.make_async_copy(tab_hbm.at[f], tab.at[f], tab_sem.at[f]).wait()
        halo_left(f).wait_recv()
        halo_right(f).wait_recv()

        def first(t, c):
            acc[t] = piece(f, t)
            return c

        def more(t, c):
            acc[t] = acc[t] + piece(f, t)
            return c

        if isinstance(f, int):
            lax.fori_loop(0, tiles, first, 0)
        else:
            lax.fori_loop(0, tiles, more, 0)
        return carry

    chunk_step(0, 0)
    lax.fori_loop(1, chunks, chunk_step, 0)

    def to_core(t):
        return remote(core_out.at[t], core_in.at[t], core_send.at[t], core_recv.at[t], seg=other)

    def to_y(t, d):
        return remote(
            y_out.at[t, d - 1], y_in.at[t, d - 1],
            y_send.at[t, d - 1], y_recv.at[t, d - 1], seg=y_peer(d),
        )

    for t in range(tiles):
        for j in range(ny):
            base = (j * CORES + (1 - mc)) * out_rows
            core_out[t, j] = acc[t, pl.ds(base, out_rows)].astype(jnp.bfloat16)
        to_core(t).start()
    for t in range(tiles):
        to_core(t).wait_recv()
        for d in list(range(1, ny)) + [0]:
            j = (my + d) % ny
            base = (j * CORES + mc) * out_rows
            val = acc[t, pl.ds(base, out_rows)] + core_in[t, j].astype(jnp.float32)
            if d:
                y_out[t, d - 1] = val.astype(jnp.bfloat16)
                to_y(t, d).start()
            else:
                y_own[t] = val
    for t in range(tiles):
        val = y_own[t]
        for d in range(1, ny):
            to_y(t, d).wait_recv()
            val = val + y_in[t, d - 1].astype(jnp.float32)
        out_ref[:, t * TILE:(t + 1) * TILE] = val

    for f in range(chunks):
        halo_left(f).wait_send()
        halo_right(f).wait_send()
    for d in range(1, NX):
        x1(d).wait_send()
        x2(d).wait_send()
    for d in range(1, nz):
        z1(d).wait_send()
        z2(d).wait_send()
    for t in range(tiles):
        to_core(t).wait_send()
        for d in range(1, ny):
            to_y(t, d).wait_send()


def solution(mesh):
    ny = mesh.shape["seg"] // CORES
    nz = mesh.shape["chan"] // NX

    def per_device(table, spectra, source_ids, pair_source, pair_offset, pair_counts):
        _, chans, _, freq = spectra.shape
        chunks = freq // BINS
        slots, n_src = pair_source.shape[0], source_ids.shape[0]
        lags = table.shape[1]
        out_rows = lags // (ny * CORES)
        tiles = slots // TILE
        pieces = chunks * 4
        step = pieces // NX
        raw = spectra.reshape(chans, 2, chunks, BINS).transpose(2, 1, 0, 3)
        ids = jnp.pad(source_ids, (0, 128 - n_src), constant_values=-1).reshape(1, 128)
        bf16, f32, dma = jnp.bfloat16, jnp.float32, pltpu.SemaphoreType.DMA
        vmem = pl.BlockSpec(memory_space=pltpu.VMEM)
        return pl.pallas_call(
            functools.partial(kernel, nz, ny),
            out_shape=jax.ShapeDtypeStruct((out_rows, slots), f32),
            in_specs=[vmem] * 5 + [pl.BlockSpec(memory_space=pl.ANY)],
            out_specs=vmem,
            scratch_shapes=[
                pltpu.VMEM((chunks, lags, 2 * BINS), bf16),
                pltpu.VMEM((chunks, 2 * BINS, 2 * chans), bf16),
                pltpu.VMEM((pieces, n_src, 128), bf16),
                pltpu.VMEM((NX - 1, step, n_src, 128), bf16),
                pltpu.VMEM((step, n_src, 128), bf16),
                pltpu.VMEM((nz - 1, step // nz, n_src, 128), bf16),
                pltpu.VMEM((pieces, n_src, 128), bf16),
                pltpu.VMEM((chunks, 2 * BINS, n_src), bf16),
                pltpu.VMEM((tiles, 2 * chans, TILE), bf16),
                pltpu.VMEM((tiles, n_src, TILE), bf16),
                pltpu.VMEM((tiles, lags, TILE), f32),
                pltpu.VMEM((tiles, ny, out_rows, TILE), bf16),
                pltpu.VMEM((tiles, ny, out_rows, TILE), bf16),
                pltpu.VMEM((tiles, ny - 1, out_rows, TILE), bf16),
                pltpu.VMEM((tiles, ny - 1, out_rows, TILE), bf16),
                pltpu.VMEM((tiles, out_rows, TILE), f32),
                dma((chunks,)),
                dma((2, chunks)), dma((2, chunks)),
                dma((NX - 1,)), dma((NX - 1,)),
                dma((nz - 1,)), dma((nz - 1,)),
                dma((nz - 1,)), dma((nz - 1,)),
                dma((NX - 1,)), dma((NX - 1,)),
                dma((tiles,)), dma((tiles,)),
                dma((tiles, ny - 1)), dma((tiles, ny - 1)),
            ],
            compiler_params=pltpu.CompilerParams(
                collective_id=0, has_side_effects=True, vmem_limit_bytes=60 << 20
            ),
            name="correlate",
        )(
            ids, pair_source.reshape(1, slots), pair_offset.reshape(1, slots),
            jnp.broadcast_to(pair_counts.reshape(1, 1), (1, slots)), raw, table,
        )

    def call(spectra, source_ids, pair_source, pair_offset, pair_counts):
        freq = spectra.shape[3]
        table = jnp.asarray(lag_table(LAGS, freq, spectra.shape[0]))
        return jax.shard_map(
            per_device, mesh=mesh,
            in_specs=(P(), P("seg", "chan", None, None), P(), P("chan"), P("chan"), P("chan")),
            out_specs=P("seg", "chan"), check_vma=False,
        )(table, spectra, source_ids, pair_source, pair_offset, pair_counts)

    return call


LAGS = 1024
```

```python
import functools
import math

import jax
import jax.numpy as jnp
import numpy as np
from jax import lax
from jax.experimental import pallas as pl
from jax.experimental.pallas import tpu as pltpu
from jax.sharding import PartitionSpec as P

MESH = pl.DeviceIdType.MESH
LAGS = 1024
WBLOCK = 64
BINS = 256
TILE = 256
CORES = 2
NX = 4
FINE = 16
PAIRS = 2
PRE = 4
SKIP = frozenset()
PACE = (1, 2, 2)


def trig_parts(lags, freq, segs):
    scale = 1.0 / math.sqrt(freq * segs)
    coarse = lags // 2 // FINE + 1
    bins = np.arange(freq, dtype=np.int64)[None, :]

    def both(tau, factor):
        theta = np.mod(tau[:, None] * bins, 2 * freq) * (math.pi / freq)
        return np.stack([np.cos(theta) * factor, np.sin(theta) * factor]).astype(np.float32)

    return both(np.arange(coarse) * FINE, scale), both(np.arange(FINE), 1.0)


def dot(a, b):
    return jnp.dot(a, b, preferred_element_type=jnp.float32)


def kernel(
    nz, ny, ids_ref, psrc_ref, poff_ref, cnt_ref, raw_hbm, coarse_ref, fine_ref, out_ref,
    raw, tab, rows, pick, slab_in, slab, part_in, srcs, hot_r, hot_s, rec, acc,
    core_out, core_in, y_out, y_in, y_own,
    raw_sem, halo_send, halo_recv, x1_send, x1_recv, z1_send, z1_recv,
    z2_send, z2_recv, x2_send, x2_recv, core_send, core_recv, y_send, y_recv,
):
    chans = raw.shape[0]
    chunks = rows.shape[0]
    band = chans // 2
    slots = psrc_ref.shape[1]
    n_src = ids_ref.shape[1]
    tiles = slots // TILE
    out_rows = out_ref.shape[0]
    half = out_rows * ny
    part_rows = pick.shape[2]
    rounds = chunks // NX
    pairs = chunks // PAIRS
    pre = min(PRE, chunks - PAIRS)
    seg, chan = lax.axis_index("seg"), lax.axis_index("chan")
    n_chan = NX * nz
    my, mc = seg // CORES, seg % CORES
    mz, mx = chan // NX, chan % NX
    left, right = (chan + n_chan - 1) % n_chan, (chan + 1) % n_chan
    other = my * CORES + (1 - mc)

    def x_peer(d):
        return mz * NX + (mx + d) % NX

    def z_peer(d):
        return ((mz + d) % nz) * NX + mx

    def y_peer(d):
        return ((my + d) % ny) * CORES + mc

    def remote(src, dst, send, recv, **where):
        return pltpu.make_async_remote_copy(
            src_ref=src, dst_ref=dst, send_sem=send, recv_sem=recv,
            device_id=where, device_id_type=MESH,
        )

    def read(f):
        cut = pl.ds(pl.multiple_of(f * BINS, BINS), BINS)
        return pltpu.make_async_copy(raw_hbm.at[:, :, cut], raw.at[:, :, cut], raw_sem.at[f])

    for f in range(chunks):
        read(f).start()

    barrier = pltpu.get_barrier_semaphore()
    met = 0
    for peer in [left, right] + [x_peer(d) for d in range(1, NX)] + [z_peer(d) for d in range(1, nz)]:
        pl.semaphore_signal(barrier, inc=1, device_id={"chan": peer}, device_id_type=MESH)
        met += 1
    for peer in [other] + [y_peer(d) for d in range(1, ny)]:
        pl.semaphore_signal(barrier, inc=1, device_id={"seg": peer}, device_id_type=MESH)
        met += 1

    def halo_left(f):
        return remote(
            rows.at[f, :, pl.ds(band, band)], rows.at[f, :, pl.ds(band + chans, band)],
            halo_send.at[0, f], halo_recv.at[0, f], chan=left,
        )

    def halo_right(f):
        return remote(
            rows.at[f, :, pl.ds(2 * band, band)], rows.at[f, :, pl.ds(0, band)],
            halo_send.at[1, f], halo_recv.at[1, f], chan=right,
        )

    local = ids_ref[...] - chan * chans
    inside = (local >= 0) & (local < chans)
    local = jnp.concatenate(
        [jnp.where(inside, local, -1), jnp.where(inside, local + chans, -1)], axis=1
    )
    chosen = jnp.where(
        lax.broadcasted_iota(jnp.int32, (2 * chans, 2 * n_src), 0) == local, 1.0, 0.0
    ).astype(jnp.bfloat16)

    def whiten(f, carry):
        read(f).wait()
        cut = pl.ds(pl.multiple_of(f * BINS, BINS), BINS)
        re, im = [jnp.transpose(raw[:, p, cut].astype(jnp.float32)) for p in range(2)]
        power = re * re + im * im
        level = jnp.mean(power.reshape(BINS // WBLOCK, WBLOCK, chans), axis=1, keepdims=True)
        inverse = jnp.broadcast_to(
            lax.rsqrt(level + 1e-06), (BINS // WBLOCK, WBLOCK, chans)
        ).reshape(BINS, chans)
        white = [(val * inverse).astype(jnp.bfloat16) for val in (re, im)]
        for p in range(2):
            rows[f, pl.ds(p * BINS, BINS), pl.ds(band, chans)] = white[p]
        got = dot(jnp.concatenate(white, axis=1), chosen).astype(jnp.bfloat16)
        for b in range(nz):
            pick[f, b] = got[b * part_rows:(b + 1) * part_rows]
        return carry

    def x1(r, d):
        return remote(
            pick.at[r * NX + (mx + d) % NX], slab_in.at[r, d - 1],
            x1_send.at[r, d - 1], x1_recv.at[r, d - 1], chan=x_peer(d),
        )

    def z1(r, d):
        return remote(
            slab.at[r, (mz + d) % nz], part_in.at[r, d - 1],
            z1_send.at[r, d - 1], z1_recv.at[r, d - 1], chan=z_peer(d),
        )

    def z2(r, d):
        return remote(
            srcs.at[r * NX + mx, mz], srcs.at[r * NX + mx, mz],
            z2_send.at[r, d - 1], z2_recv.at[r, d - 1], chan=z_peer(d),
        )

    def x2(r, d):
        return remote(
            srcs.at[r * NX + mx], srcs.at[r * NX + mx],
            x2_send.at[r, d - 1], x2_recv.at[r, d - 1], chan=x_peer(d),
        )

    lax.fori_loop(0, chunks, whiten, 0)
    pl.semaphore_wait(barrier, met)
    for r in range(rounds):
        for d in range(1, NX):
            x1(r, d).start()

    def send_halo(f, carry):
        halo_left(f).start()
        halo_right(f).start()
        return carry

    paces = [min(sum(PACE[:i]), chunks) for i in range(len(PACE) + 1)] + [chunks]

    def send_some(stage):
        if "halo" not in SKIP:
            lax.fori_loop(paces[stage], paces[stage + 1], send_halo, 0)

    send_some(0)

    def hots():
        at = poff_ref[...] + band
        live = lax.broadcasted_iota(jnp.int32, (1, slots), 1) < cnt_ref[...]
        src_at = jnp.where(live, psrc_ref[...], -4 * n_src)
        for t in range(tiles):
            cut = slice(t * TILE, (t + 1) * TILE)
            hot_r[t] = jnp.where(
                lax.broadcasted_iota(jnp.int32, (2 * chans, TILE), 0) == at[:, cut], 1.0, 0.0
            ).astype(jnp.bfloat16)
            for p in range(2):
                hot_s[t, p] = jnp.where(
                    lax.broadcasted_iota(jnp.int32, (2 * n_src, TILE), 0)
                    == src_at[:, cut] + p * n_src, 1.0, 0.0
                ).astype(jnp.bfloat16)

    def table(i, carry):
        at = pl.ds(pl.multiple_of(i * FINE, FINE), FINE)
        for f in range(chunks):
            cut = pl.ds(f * BINS, BINS)
            c1, s1 = coarse_ref[0, pl.ds(i, 1), cut], coarse_ref[1, pl.ds(i, 1), cut]
            c2, s2 = fine_ref[0, :, cut], fine_ref[1, :, cut]
            place = pl.ds(f % PAIRS * BINS, BINS)
            tab[f // PAIRS, 0, at, place] = (c1 * c2 - s1 * s2).astype(jnp.bfloat16)
            tab[f // PAIRS, 1, at, place] = (s1 * c2 + c1 * s2).astype(jnp.bfloat16)
        return carry

    def gather(f):
        wait_halo(f)
        for t in range(tiles):
            rec[t, f] = dot(rows[f], hot_r[t]).astype(jnp.bfloat16)

    def gather_step(f, carry):
        gather(f)
        return carry

    def wait_halo(f):
        halo_left(f).wait_recv()
        halo_right(f).wait_recv()

    hots()
    lax.fori_loop(0, coarse_ref.shape[1], table, 0)
    acc[...] = jnp.zeros_like(acc)
    for r in range(rounds):
        for d in range(1, NX):
            x1(r, d).wait_recv()
        total = pick[r * NX + mx]
        for d in range(1, NX):
            total = total + slab_in[r, d - 1]
        slab[r] = total
        for d in range(1, nz):
            z1(r, d).start()
    send_some(1)
    for r in range(rounds):
        for d in range(1, nz):
            z1(r, d).wait_recv()
        total = slab[r, mz]
        for d in range(1, nz):
            total = total + part_in[r, d - 1]
        srcs[r * NX + mx, mz] = total
        for d in range(1, nz):
            z2(r, d).start()
    send_some(2)
    for r in range(rounds):
        for d in range(1, nz):
            z2(r, d).wait_recv()
        for d in range(1, NX):
            x2(r, d).start()
    send_some(3)
    lax.fori_loop(0, pre, gather_step, 0)

    def cross(f, t, early):
        got = rec[t, f].astype(jnp.float32) if early else dot(rows[f], hot_r[t])
        lhs = srcs[f].reshape(BINS, 2 * n_src)
        sr, si = dot(lhs, hot_s[t, 0]), dot(lhs, hot_s[t, 1])
        rr, ri = got[:BINS], got[BINS:]
        real, imag = sr * rr + si * ri, si * rr - sr * ri
        return real.astype(jnp.bfloat16), imag.astype(jnp.bfloat16)

    def wait_sources(r):
        for d in range(1, NX):
            x2(r, d).wait_recv()

    def pair_sum(i, t, early):
        vals = [cross(i * PAIRS + k, t, early) for k in range(PAIRS)]
        return [
            acc[t, p] + dot(tab[i, p], jnp.concatenate([v[p] for v in vals], axis=0))
            for p in range(2)
        ]

    def pair_step(early):
        def run(i, carry):
            if not early:
                for k in range(PAIRS):
                    wait_halo(i * PAIRS + k)
            for t in range(tiles):
                acc[t, 0], acc[t, 1] = pair_sum(i, t, early)
            return carry
        return run

    for r in range(rounds):
        if r * NX // PAIRS < pairs - 1:
            wait_sources(r)
        for early in (True, False):
            low, high = r * NX // PAIRS, min((r + 1) * NX // PAIRS, pairs - 1)
            if early:
                high = min(high, pre // PAIRS)
            else:
                low = max(low, pre // PAIRS)
            if low < high:
                lax.fori_loop(low, high, pair_step(early), 0)
    if (rounds - 1) * NX // PAIRS >= pairs - 1:
        wait_sources(rounds - 1)
    for k in range(PAIRS):
        wait_halo((pairs - 1) * PAIRS + k)

    def to_core(t):
        return remote(core_out.at[t], core_in.at[t], core_send.at[t], core_recv.at[t], seg=other)

    def to_y(t, d):
        return remote(
            y_out.at[t, d - 1], y_in.at[t, d - 1],
            y_send.at[t, d - 1], y_recv.at[t, d - 1], seg=y_peer(d),
        )

    def lag_block(t, j, parity):
        block = j * CORES + parity
        if j >= ny // 2:
            at = pl.ds(pl.multiple_of(block * out_rows - half, out_rows), out_rows)
            return acc[t, 0, at] - acc[t, 1, at]
        at = pl.ds(pl.multiple_of(half - (block + 1) * out_rows, out_rows), out_rows + 8)
        return (acc[t, 0, at] + acc[t, 1, at])[1:out_rows + 1]

    def finish_tile(t):
        acc[t, 0], acc[t, 1] = pair_sum(pairs - 1, t, False)
        if "rs" in SKIP:
            return
        for j in range(ny):
            core_out[t, j] = lag_block(t, j, 1 - mc).astype(jnp.bfloat16)
        to_core(t).start()

    def pass_on(t):
        to_core(t).wait_recv()
        for j in range(ny):
            y_own[t, j] = lag_block(t, j, mc) + core_in[t, j].astype(jnp.float32)
        for d in range(1, ny):
            y_out[t, d - 1] = y_own[t, (my + d) % ny].astype(jnp.bfloat16)
            to_y(t, d).start()

    for t in range(tiles):
        finish_tile(t)
        if t and "rs" not in SKIP:
            pass_on(t - 1)
    if "rs" not in SKIP:
        pass_on(tiles - 1)

    place = lax.broadcasted_iota(jnp.int32, (out_rows, out_rows), 0)
    place = jnp.where(my >= ny // 2, place, out_rows - 1 - place)
    order = jnp.where(
        lax.broadcasted_iota(jnp.int32, (out_rows, out_rows), 1) == place, 1.0, 0.0
    ).astype(jnp.bfloat16)
    for t in range(tiles):
        val = y_own[t, my]
        if "rs" not in SKIP:
            for d in range(1, ny):
                to_y(t, d).wait_recv()
                val = val + y_in[t, d - 1].astype(jnp.float32)
        high = val.astype(jnp.bfloat16)
        rest = val - high.astype(jnp.float32)
        mid = rest.astype(jnp.bfloat16)
        low = (rest - mid.astype(jnp.float32)).astype(jnp.bfloat16)
        out_ref[:, t * TILE:(t + 1) * TILE] = dot(order, high) + (dot(order, mid) + dot(order, low))

    def halo_sent(f, carry):
        halo_left(f).wait_send()
        halo_right(f).wait_send()
        return carry

    if "halo" not in SKIP:
        lax.fori_loop(0, chunks, halo_sent, 0)
    for r in range(rounds):
        for d in range(1, NX):
            x1(r, d).wait_send()
            x2(r, d).wait_send()
        for d in range(1, nz):
            z1(r, d).wait_send()
            z2(r, d).wait_send()
    if "rs" not in SKIP:
        for t in range(tiles):
            to_core(t).wait_send()
            for d in range(1, ny):
                to_y(t, d).wait_send()


def solution(mesh):
    ny = mesh.shape["seg"] // CORES
    nz = mesh.shape["chan"] // NX

    def per_device(coarse, fine, spectra, source_ids, pair_source, pair_offset, pair_counts):
        _, chans, _, freq = spectra.shape
        chunks = freq // BINS
        slots, n_src = pair_source.shape[0], source_ids.shape[0]
        out_rows = LAGS // (ny * CORES)
        tiles = slots // TILE
        rounds = chunks // NX
        part = (BINS // nz, 2 * n_src)
        taus = coarse.shape[1] * FINE
        bf16, f32, dma = jnp.bfloat16, jnp.float32, pltpu.SemaphoreType.DMA
        vmem = pl.BlockSpec(memory_space=pltpu.VMEM)
        return pl.pallas_call(
            functools.partial(kernel, nz, ny),
            out_shape=jax.ShapeDtypeStruct((out_rows, slots), f32),
            in_specs=[vmem] * 4 + [pl.BlockSpec(memory_space=pl.ANY)] + [vmem] * 2,
            out_specs=vmem,
            scratch_shapes=[
                pltpu.VMEM((chans, 2, freq), bf16),
                pltpu.VMEM((chunks // PAIRS, 2, taus, PAIRS * BINS), bf16),
                pltpu.VMEM((chunks, 2 * BINS, 2 * chans), bf16),
                pltpu.VMEM((chunks, nz, *part), bf16),
                pltpu.VMEM((rounds, NX - 1, nz, *part), bf16),
                pltpu.VMEM((rounds, nz, *part), bf16),
                pltpu.VMEM((rounds, nz - 1, *part), bf16),
                pltpu.VMEM((chunks, nz, *part), bf16),
                pltpu.VMEM((tiles, 2 * chans, TILE), bf16),
                pltpu.VMEM((tiles, 2, 2 * n_src, TILE), bf16),
                pltpu.VMEM((tiles, PRE, 2 * BINS, TILE), bf16),
                pltpu.VMEM((tiles, 2, taus, TILE), f32),
                pltpu.VMEM((tiles, ny, out_rows, TILE), bf16),
                pltpu.VMEM((tiles, ny, out_rows, TILE), bf16),
                pltpu.VMEM((tiles, ny - 1, out_rows, TILE), bf16),
                pltpu.VMEM((tiles, ny - 1, out_rows, TILE), bf16),
                pltpu.VMEM((tiles, ny, out_rows, TILE), f32),
                dma((chunks,)),
                dma((2, chunks)), dma((2, chunks)),
                dma((rounds, NX - 1)), dma((rounds, NX - 1)),
                dma((rounds, nz - 1)), dma((rounds, nz - 1)),
                dma((rounds, nz - 1)), dma((rounds, nz - 1)),
                dma((rounds, NX - 1)), dma((rounds, NX - 1)),
                dma((tiles,)), dma((tiles,)),
                dma((tiles, ny - 1)), dma((tiles, ny - 1)),
            ],
            compiler_params=pltpu.CompilerParams(
                collective_id=0, has_side_effects=True, vmem_limit_bytes=58 << 20
            ),
            name="correlate",
        )(
            source_ids.reshape(1, n_src), pair_source.reshape(1, slots),
            pair_offset.reshape(1, slots), pair_counts.reshape(1, 1), spectra[0], coarse, fine,
        )

    def call(spectra, source_ids, pair_source, pair_offset, pair_counts):
        coarse, fine = trig_parts(LAGS, spectra.shape[3], spectra.shape[0])
        return jax.shard_map(
            per_device, mesh=mesh,
            in_specs=(
                P(), P(), P("seg", "chan", None, None), P(), P("chan"), P("chan"), P("chan")
            ),
            out_specs=P("seg", "chan"), check_vma=False,
        )(
            jnp.asarray(coarse), jnp.asarray(fine),
            spectra, source_ids, pair_source, pair_offset, pair_counts,
        )

    return call
```

```python
import functools
import math

import jax
import jax.numpy as jnp
import numpy as np
from jax import lax
from jax.experimental import pallas as pl
from jax.experimental.pallas import tpu as pltpu
from jax.sharding import PartitionSpec as P

MESH = pl.DeviceIdType.MESH
LAGS = 1024
WBLOCK = 64
BINS = 256
TILE = 256
CORES = 2
NX = 4
FINE = 16
PAIRS = 2
PRE = 4
SKIP = frozenset()
PACE = (1, 1, 0, 1, 0, 0, 0)
AHEAD = 2


def trig_parts(lags, freq, segs):
    scale = 1.0 / math.sqrt(freq * segs)
    coarse = lags // 2 // FINE + 1
    bins = np.arange(freq, dtype=np.int64)[None, :]

    def both(tau, factor):
        theta = np.mod(tau[:, None] * bins, 2 * freq) * (math.pi / freq)
        return np.stack([np.cos(theta) * factor, np.sin(theta) * factor]).astype(np.float32)

    return both(np.arange(coarse) * FINE, scale), both(np.arange(FINE), 1.0)


def dot(a, b):
    return jnp.dot(a, b, preferred_element_type=jnp.float32)


def kernel(
    nz, ny, ids_ref, psrc_ref, poff_ref, cnt_ref, raw_hbm, coarse_ref, fine_ref, out_ref,
    raw, tab, rows, pick, slab_in, slab, part_in, srcs, hot_r, hot_s, rec, acc,
    core_out, core_in, y_out, y_in, y_own,
    raw_sem, halo_send, halo_recv, x1_send, x1_recv, z1_send, z1_recv,
    z2_send, z2_recv, x2_send, x2_recv, core_send, core_recv, y_send, y_recv,
):
    chans = raw.shape[0]
    chunks = rows.shape[0]
    band = chans // 2
    slots = psrc_ref.shape[1]
    n_src = ids_ref.shape[1]
    tiles = slots // TILE
    out_rows = out_ref.shape[0]
    half = out_rows * ny
    part_rows = pick.shape[2]
    rounds = chunks // NX
    pairs = chunks // PAIRS
    pre = min(PRE, chunks - PAIRS)
    seg, chan = lax.axis_index("seg"), lax.axis_index("chan")
    n_chan = NX * nz
    my, mc = seg // CORES, seg % CORES
    mz, mx = chan // NX, chan % NX
    left, right = (chan + n_chan - 1) % n_chan, (chan + 1) % n_chan
    other = my * CORES + (1 - mc)

    def x_peer(d):
        return mz * NX + (mx + d) % NX

    def z_peer(d):
        return ((mz + d) % nz) * NX + mx

    def y_peer(d):
        return ((my + d) % ny) * CORES + mc

    def remote(src, dst, send, recv, **where):
        return pltpu.make_async_remote_copy(
            src_ref=src, dst_ref=dst, send_sem=send, recv_sem=recv,
            device_id=where, device_id_type=MESH,
        )

    def read(f):
        cut = pl.ds(pl.multiple_of(f * BINS, BINS), BINS)
        return pltpu.make_async_copy(raw_hbm.at[:, :, cut], raw.at[:, :, cut], raw_sem.at[f])

    for f in range(chunks):
        read(f).start()

    barrier = pltpu.get_barrier_semaphore()
    met = 0
    for peer in [left, right] + [x_peer(d) for d in range(1, NX)] + [z_peer(d) for d in range(1, nz)]:
        pl.semaphore_signal(barrier, inc=1, device_id={"chan": peer}, device_id_type=MESH)
        met += 1
    for peer in [other] + [y_peer(d) for d in range(1, ny)]:
        pl.semaphore_signal(barrier, inc=1, device_id={"seg": peer}, device_id_type=MESH)
        met += 1

    def halo_left(f):
        return remote(
            rows.at[f, :, pl.ds(band, band)], rows.at[f, :, pl.ds(band + chans, band)],
            halo_send.at[0, f], halo_recv.at[0, f], chan=left,
        )

    def halo_right(f):
        return remote(
            rows.at[f, :, pl.ds(2 * band, band)], rows.at[f, :, pl.ds(0, band)],
            halo_send.at[1, f], halo_recv.at[1, f], chan=right,
        )

    local = ids_ref[...] - chan * chans
    inside = (local >= 0) & (local < chans)
    local = jnp.concatenate(
        [jnp.where(inside, local, -1), jnp.where(inside, local + chans, -1)], axis=1
    )
    chosen = jnp.where(
        lax.broadcasted_iota(jnp.int32, (2 * chans, 2 * n_src), 0) == local, 1.0, 0.0
    ).astype(jnp.bfloat16)

    def whiten(f, carry):
        read(f).wait()
        cut = pl.ds(pl.multiple_of(f * BINS, BINS), BINS)
        re, im = [jnp.transpose(raw[:, p, cut].astype(jnp.float32)) for p in range(2)]
        power = re * re + im * im
        level = jnp.mean(power.reshape(BINS // WBLOCK, WBLOCK, chans), axis=1, keepdims=True)
        inverse = jnp.broadcast_to(
            lax.rsqrt(level + 1e-06), (BINS // WBLOCK, WBLOCK, chans)
        ).reshape(BINS, chans)
        white = [(val * inverse).astype(jnp.bfloat16) for val in (re, im)]
        for p in range(2):
            rows[f, pl.ds(p * BINS, BINS), pl.ds(band, chans)] = white[p]
        got = dot(jnp.concatenate(white, axis=1), chosen).astype(jnp.bfloat16)
        for b in range(nz):
            pick[f, b] = got[b * part_rows:(b + 1) * part_rows]
        return carry

    def x1(r, d):
        return remote(
            pick.at[r * NX + (mx + d) % NX], slab_in.at[r, d - 1],
            x1_send.at[r, d - 1], x1_recv.at[r, d - 1], chan=x_peer(d),
        )

    def z1(r, d):
        return remote(
            slab.at[r, (mz + d) % nz], part_in.at[r, d - 1],
            z1_send.at[r, d - 1], z1_recv.at[r, d - 1], chan=z_peer(d),
        )

    def z2(r, d):
        return remote(
            srcs.at[r * NX + mx, mz], srcs.at[r * NX + mx, mz],
            z2_send.at[r, d - 1], z2_recv.at[r, d - 1], chan=z_peer(d),
        )

    def x2(r, d):
        return remote(
            srcs.at[r * NX + mx], srcs.at[r * NX + mx],
            x2_send.at[r, d - 1], x2_recv.at[r, d - 1], chan=x_peer(d),
        )

    for r in range(rounds):
        lax.fori_loop(r * NX, (r + 1) * NX, whiten, 0)
        if r == 0:
            pl.semaphore_wait(barrier, met)
        for d in range(1, NX):
            x1(r, d).start()

    fed = [0]

    def feed(count):
        for _ in range(count):
            f = fed[0]
            if f == chunks:
                return
            if f >= AHEAD:
                sent_halo(f - AHEAD)
            halo_left(f).start()
            halo_right(f).start()
            fed[0] += 1

    def sent_halo(f):
        halo_left(f).wait_send()
        halo_right(f).wait_send()

    paces = list(PACE)
    feed(paces.pop(0))

    def hots():
        at = poff_ref[...] + band
        live = lax.broadcasted_iota(jnp.int32, (1, slots), 1) < cnt_ref[...]
        src_at = jnp.where(live, psrc_ref[...], -4 * n_src)
        for t in range(tiles):
            cut = slice(t * TILE, (t + 1) * TILE)
            hot_r[t] = jnp.where(
                lax.broadcasted_iota(jnp.int32, (2 * chans, TILE), 0) == at[:, cut], 1.0, 0.0
            ).astype(jnp.bfloat16)
            for p in range(2):
                hot_s[t, p] = jnp.where(
                    lax.broadcasted_iota(jnp.int32, (2 * n_src, TILE), 0)
                    == src_at[:, cut] + p * n_src, 1.0, 0.0
                ).astype(jnp.bfloat16)

    def table(i, carry):
        at = pl.ds(pl.multiple_of(i * FINE, FINE), FINE)
        for f in range(chunks):
            cut = pl.ds(f * BINS, BINS)
            c1, s1 = coarse_ref[0, pl.ds(i, 1), cut], coarse_ref[1, pl.ds(i, 1), cut]
            c2, s2 = fine_ref[0, :, cut], fine_ref[1, :, cut]
            place = pl.ds(f % PAIRS * BINS, BINS)
            tab[f // PAIRS, 0, at, place] = (c1 * c2 - s1 * s2).astype(jnp.bfloat16)
            tab[f // PAIRS, 1, at, place] = (s1 * c2 + c1 * s2).astype(jnp.bfloat16)
        return carry

    def gather(f):
        wait_halo(f)
        for t in range(tiles):
            rec[t, f] = dot(rows[f], hot_r[t]).astype(jnp.bfloat16)

    def wait_halo(f):
        halo_left(f).wait_recv()
        halo_right(f).wait_recv()

    hots()
    lax.fori_loop(0, coarse_ref.shape[1], table, 0)
    acc[...] = jnp.zeros_like(acc)
    for r in range(rounds):
        for d in range(1, NX):
            x1(r, d).wait_recv()
        total = pick[r * NX + mx]
        for d in range(1, NX):
            total = total + slab_in[r, d - 1]
        slab[r] = total
        for d in range(1, nz):
            z1(r, d).start()
        feed(paces.pop(0))
    for r in range(rounds):
        for d in range(1, nz):
            z1(r, d).wait_recv()
        total = slab[r, mz]
        for d in range(1, nz):
            total = total + part_in[r, d - 1]
        srcs[r * NX + mx, mz] = total
        for d in range(1, nz):
            z2(r, d).start()
        feed(paces.pop(0))
    for r in range(rounds):
        for d in range(1, nz):
            z2(r, d).wait_recv()
        for d in range(1, NX):
            x2(r, d).start()
        feed(paces.pop(0))
    for f in range(pre):
        gather(f)
        feed(1)

    def cross(f, t, early):
        got = rec[t, f].astype(jnp.float32) if early else dot(rows[f], hot_r[t])
        lhs = srcs[f].reshape(BINS, 2 * n_src)
        sr, si = dot(lhs, hot_s[t, 0]), dot(lhs, hot_s[t, 1])
        rr, ri = got[:BINS], got[BINS:]
        real, imag = sr * rr + si * ri, si * rr - sr * ri
        return real.astype(jnp.bfloat16), imag.astype(jnp.bfloat16)

    def wait_sources(r):
        for d in range(1, NX):
            x2(r, d).wait_recv()

    def pair_sum(i, t, early):
        vals = [cross(i * PAIRS + k, t, early) for k in range(PAIRS)]
        return [
            acc[t, p] + dot(tab[i, p], jnp.concatenate([v[p] for v in vals], axis=0))
            for p in range(2)
        ]

    def pair_step(early):
        def run(i, carry):
            if not early:
                for k in range(PAIRS):
                    wait_halo(i * PAIRS + k)
            for t in range(tiles):
                acc[t, 0], acc[t, 1] = pair_sum(i, t, early)
            return carry
        return run

    for r in range(rounds):
        if r * NX // PAIRS < pairs - 1:
            wait_sources(r)
        for early in (True, False):
            low, high = r * NX // PAIRS, min((r + 1) * NX // PAIRS, pairs - 1)
            if early:
                high = min(high, pre // PAIRS)
            else:
                low = max(low, pre // PAIRS)
            if low < high:
                for i in range(low, high):
                    pair_step(early)(i, 0)
                    feed(1)
    feed(chunks)
    if (rounds - 1) * NX // PAIRS >= pairs - 1:
        wait_sources(rounds - 1)
    for k in range(PAIRS):
        wait_halo((pairs - 1) * PAIRS + k)

    def to_core(t):
        return remote(core_out.at[t], core_in.at[t], core_send.at[t], core_recv.at[t], seg=other)

    def to_y(t, d):
        return remote(
            y_out.at[t, d - 1], y_in.at[t, d - 1],
            y_send.at[t, d - 1], y_recv.at[t, d - 1], seg=y_peer(d),
        )

    def lag_block(t, j, parity):
        block = j * CORES + parity
        if j >= ny // 2:
            at = pl.ds(pl.multiple_of(block * out_rows - half, out_rows), out_rows)
            return acc[t, 0, at] - acc[t, 1, at]
        at = pl.ds(pl.multiple_of(half - (block + 1) * out_rows, out_rows), out_rows + 8)
        return (acc[t, 0, at] + acc[t, 1, at])[1:out_rows + 1]

    def finish_tile(t):
        acc[t, 0], acc[t, 1] = pair_sum(pairs - 1, t, False)
        if "rs" in SKIP:
            return
        for j in range(ny):
            core_out[t, j] = lag_block(t, j, 1 - mc).astype(jnp.bfloat16)
        to_core(t).start()

    def pass_on(t):
        to_core(t).wait_recv()
        for j in range(ny):
            y_own[t, j] = lag_block(t, j, mc) + core_in[t, j].astype(jnp.float32)
        for d in range(1, ny):
            y_out[t, d - 1] = y_own[t, (my + d) % ny].astype(jnp.bfloat16)
            to_y(t, d).start()

    for t in range(tiles):
        finish_tile(t)
        if t and "rs" not in SKIP:
            pass_on(t - 1)
    if "rs" not in SKIP:
        pass_on(tiles - 1)

    place = lax.broadcasted_iota(jnp.int32, (out_rows, out_rows), 0)
    place = jnp.where(my >= ny // 2, place, out_rows - 1 - place)
    order = jnp.where(
        lax.broadcasted_iota(jnp.int32, (out_rows, out_rows), 1) == place, 1.0, 0.0
    ).astype(jnp.bfloat16)
    for t in range(tiles):
        val = y_own[t, my]
        if "rs" not in SKIP:
            for d in range(1, ny):
                to_y(t, d).wait_recv()
                val = val + y_in[t, d - 1].astype(jnp.float32)
        high = val.astype(jnp.bfloat16)
        rest = val - high.astype(jnp.float32)
        mid = rest.astype(jnp.bfloat16)
        low = (rest - mid.astype(jnp.float32)).astype(jnp.bfloat16)
        out_ref[:, t * TILE:(t + 1) * TILE] = dot(order, high) + (dot(order, mid) + dot(order, low))

    for f in range(max(0, chunks - AHEAD), chunks):
        sent_halo(f)
    for r in range(rounds):
        for d in range(1, NX):
            x1(r, d).wait_send()
            x2(r, d).wait_send()
        for d in range(1, nz):
            z1(r, d).wait_send()
            z2(r, d).wait_send()
    if "rs" not in SKIP:
        for t in range(tiles):
            to_core(t).wait_send()
            for d in range(1, ny):
                to_y(t, d).wait_send()


def solution(mesh):
    ny = mesh.shape["seg"] // CORES
    nz = mesh.shape["chan"] // NX

    def per_device(coarse, fine, spectra, source_ids, pair_source, pair_offset, pair_counts):
        _, chans, _, freq = spectra.shape
        chunks = freq // BINS
        slots, n_src = pair_source.shape[0], source_ids.shape[0]
        out_rows = LAGS // (ny * CORES)
        tiles = slots // TILE
        rounds = chunks // NX
        part = (BINS // nz, 2 * n_src)
        taus = coarse.shape[1] * FINE
        bf16, f32, dma = jnp.bfloat16, jnp.float32, pltpu.SemaphoreType.DMA
        vmem = pl.BlockSpec(memory_space=pltpu.VMEM)
        return pl.pallas_call(
            functools.partial(kernel, nz, ny),
            out_shape=jax.ShapeDtypeStruct((out_rows, slots), f32),
            in_specs=[vmem] * 4 + [pl.BlockSpec(memory_space=pl.ANY)] + [vmem] * 2,
            out_specs=vmem,
            scratch_shapes=[
                pltpu.VMEM((chans, 2, freq), bf16),
                pltpu.VMEM((chunks // PAIRS, 2, taus, PAIRS * BINS), bf16),
                pltpu.VMEM((chunks, 2 * BINS, 2 * chans), bf16),
                pltpu.VMEM((chunks, nz, *part), bf16),
                pltpu.VMEM((rounds, NX - 1, nz, *part), bf16),
                pltpu.VMEM((rounds, nz, *part), bf16),
                pltpu.VMEM((rounds, nz - 1, *part), bf16),
                pltpu.VMEM((chunks, nz, *part), bf16),
                pltpu.VMEM((tiles, 2 * chans, TILE), bf16),
                pltpu.VMEM((tiles, 2, 2 * n_src, TILE), bf16),
                pltpu.VMEM((tiles, PRE, 2 * BINS, TILE), bf16),
                pltpu.VMEM((tiles, 2, taus, TILE), f32),
                pltpu.VMEM((tiles, ny, out_rows, TILE), bf16),
                pltpu.VMEM((tiles, ny, out_rows, TILE), bf16),
                pltpu.VMEM((tiles, ny - 1, out_rows, TILE), bf16),
                pltpu.VMEM((tiles, ny - 1, out_rows, TILE), bf16),
                pltpu.VMEM((tiles, ny, out_rows, TILE), f32),
                dma((chunks,)),
                dma((2, chunks)), dma((2, chunks)),
                dma((rounds, NX - 1)), dma((rounds, NX - 1)),
                dma((rounds, nz - 1)), dma((rounds, nz - 1)),
                dma((rounds, nz - 1)), dma((rounds, nz - 1)),
                dma((rounds, NX - 1)), dma((rounds, NX - 1)),
                dma((tiles,)), dma((tiles,)),
                dma((tiles, ny - 1)), dma((tiles, ny - 1)),
            ],
            compiler_params=pltpu.CompilerParams(
                collective_id=0, has_side_effects=True, vmem_limit_bytes=58 << 20
            ),
            name="correlate",
        )(
            source_ids.reshape(1, n_src), pair_source.reshape(1, slots),
            pair_offset.reshape(1, slots), pair_counts.reshape(1, 1), spectra[0], coarse, fine,
        )

    def call(spectra, source_ids, pair_source, pair_offset, pair_counts):
        coarse, fine = trig_parts(LAGS, spectra.shape[3], spectra.shape[0])
        return jax.shard_map(
            per_device, mesh=mesh,
            in_specs=(
                P(), P(), P("seg", "chan", None, None), P(), P("chan"), P("chan"), P("chan")
            ),
            out_specs=P("seg", "chan"), check_vma=False,
        )(
            jnp.asarray(coarse), jnp.asarray(fine),
            spectra, source_ids, pair_source, pair_offset, pair_counts,
        )

    return call
```

```python
import functools
import math

import jax
import jax.numpy as jnp
import numpy as np
from jax import lax
from jax.experimental import pallas as pl
from jax.experimental.pallas import tpu as pltpu
from jax.sharding import PartitionSpec as P

MESH = pl.DeviceIdType.MESH
LAGS = 1024
WBLOCK = 64
BINS = 256
TILE = 256
CORES = 2
NX = 4
FINE = 16
PAIRS = 2
PRE = 4
PACE = (1, 1, 0, 1, 0, 0, 0)
AHEAD = 2


def trig_parts(lags, freq, segs):
    scale = 1.0 / math.sqrt(freq * segs)
    coarse = lags // 2 // FINE + 1
    bins = np.arange(freq, dtype=np.int64)[None, :]

    def both(tau, factor):
        theta = np.mod(tau[:, None] * bins, 2 * freq) * (math.pi / freq)
        return np.stack([np.cos(theta) * factor, np.sin(theta) * factor]).astype(np.float32)

    return both(np.arange(coarse) * FINE, scale), both(np.arange(FINE), 1.0)


def dot(a, b):
    return jnp.dot(a, b, preferred_element_type=jnp.float32)


def kernel(
    nz, ny, ids_ref, psrc_ref, poff_ref, cnt_ref, raw_hbm, coarse_ref, fine_ref, out_ref,
    raw, tab, rows, pick, slab_in, slab, part_in, srcs, hot_r, hot_s, rec, acc,
    core_out, core_in, relay_out, relay_in, y_out, y_in, y_own,
    raw_sem, halo_send, halo_recv, x1_send, x1_recv, z1_send, z1_recv,
    z2_send, z2_recv, x2_send, x2_recv, core_send, core_recv, relay_send, relay_recv, y_send, y_recv,
):
    chans = raw.shape[0]
    chunks = rows.shape[0]
    band = chans // 2
    slots = psrc_ref.shape[1]
    n_src = ids_ref.shape[1]
    tiles = slots // TILE
    out_rows = out_ref.shape[0]
    half = out_rows * ny
    part_rows = pick.shape[2]
    rounds = chunks // NX
    pairs = chunks // PAIRS
    pre = min(PRE, chunks - PAIRS)
    seg, chan = lax.axis_index("seg"), lax.axis_index("chan")
    n_chan = NX * nz
    my, mc = seg // CORES, seg % CORES
    mz, mx = chan // NX, chan % NX
    left, right = (chan + n_chan - 1) % n_chan, (chan + 1) % n_chan
    other = my * CORES + (1 - mc)

    def x_peer(d):
        return mz * NX + (mx + d) % NX

    def z_peer(d):
        return ((mz + d) % nz) * NX + mx

    def y_peer(d):
        return ((my + d) % ny) * CORES + mc

    def remote(src, dst, send, recv, **where):
        return pltpu.make_async_remote_copy(
            src_ref=src, dst_ref=dst, send_sem=send, recv_sem=recv,
            device_id=where, device_id_type=MESH,
        )

    def read(f):
        cut = pl.ds(pl.multiple_of(f * BINS, BINS), BINS)
        return pltpu.make_async_copy(raw_hbm.at[:, :, cut], raw.at[:, :, cut], raw_sem.at[f])

    for f in range(chunks):
        read(f).start()

    barrier = pltpu.get_barrier_semaphore()
    met = 0
    for peer in [left, right] + [x_peer(d) for d in range(1, NX)] + [z_peer(d) for d in range(1, nz)]:
        pl.semaphore_signal(barrier, inc=1, device_id={"chan": peer}, device_id_type=MESH)
        met += 1
    for peer in [other] + [y_peer(d) for d in range(1, ny)]:
        pl.semaphore_signal(barrier, inc=1, device_id={"seg": peer}, device_id_type=MESH)
        met += 1

    def halo_left(f):
        return remote(
            rows.at[f, :, pl.ds(band, band)], rows.at[f, :, pl.ds(band + chans, band)],
            halo_send.at[0, f], halo_recv.at[0, f], chan=left,
        )

    def halo_right(f):
        return remote(
            rows.at[f, :, pl.ds(2 * band, band)], rows.at[f, :, pl.ds(0, band)],
            halo_send.at[1, f], halo_recv.at[1, f], chan=right,
        )

    local = ids_ref[...] - chan * chans
    inside = (local >= 0) & (local < chans)
    local = jnp.concatenate(
        [jnp.where(inside, local, -1), jnp.where(inside, local + chans, -1)], axis=1
    )
    chosen = jnp.where(
        lax.broadcasted_iota(jnp.int32, (2 * chans, 2 * n_src), 0) == local, 1.0, 0.0
    ).astype(jnp.bfloat16)

    def whiten(f, carry):
        read(f).wait()
        cut = pl.ds(pl.multiple_of(f * BINS, BINS), BINS)
        re, im = [jnp.transpose(raw[:, p, cut].astype(jnp.float32)) for p in range(2)]
        power = re * re + im * im
        level = jnp.mean(power.reshape(BINS // WBLOCK, WBLOCK, chans), axis=1, keepdims=True)
        inverse = jnp.broadcast_to(
            lax.rsqrt(level + 1e-06), (BINS // WBLOCK, WBLOCK, chans)
        ).reshape(BINS, chans)
        white = [(val * inverse).astype(jnp.bfloat16) for val in (re, im)]
        for p in range(2):
            rows[f, pl.ds(p * BINS, BINS), pl.ds(band, chans)] = white[p]
        got = dot(jnp.concatenate(white, axis=1), chosen).astype(jnp.bfloat16)
        for b in range(nz):
            pick[f, b] = got[b * part_rows:(b + 1) * part_rows]
        return carry

    def x1(r, d):
        return remote(
            pick.at[r * NX + (mx + d) % NX], slab_in.at[r, d - 1],
            x1_send.at[r, d - 1], x1_recv.at[r, d - 1], chan=x_peer(d),
        )

    def z1(r, d):
        return remote(
            slab.at[r, (mz + d) % nz], part_in.at[r, d - 1],
            z1_send.at[r, d - 1], z1_recv.at[r, d - 1], chan=z_peer(d),
        )

    def z2(r, d):
        return remote(
            srcs.at[r * NX + mx, mz], srcs.at[r * NX + mx, mz],
            z2_send.at[r, d - 1], z2_recv.at[r, d - 1], chan=z_peer(d),
        )

    def x2(r, d):
        return remote(
            srcs.at[r * NX + mx], srcs.at[r * NX + mx],
            x2_send.at[r, d - 1], x2_recv.at[r, d - 1], chan=x_peer(d),
        )

    for r in range(rounds):
        lax.fori_loop(r * NX, (r + 1) * NX, whiten, 0)
        if r == 0:
            pl.semaphore_wait(barrier, met)
        for d in range(1, NX):
            x1(r, d).start()

    fed = [0]

    def feed(count):
        for _ in range(count):
            f = fed[0]
            if f == chunks:
                return
            if f >= AHEAD:
                sent_halo(f - AHEAD)
            halo_left(f).start()
            halo_right(f).start()
            fed[0] += 1

    def sent_halo(f):
        halo_left(f).wait_send()
        halo_right(f).wait_send()

    paces = list(PACE)
    feed(paces.pop(0))

    def hots():
        at = poff_ref[...] + band
        live = lax.broadcasted_iota(jnp.int32, (1, slots), 1) < cnt_ref[...]
        src_at = jnp.where(live, psrc_ref[...], -4 * n_src)
        for t in range(tiles):
            cut = slice(t * TILE, (t + 1) * TILE)
            hot_r[t] = jnp.where(
                lax.broadcasted_iota(jnp.int32, (2 * chans, TILE), 0) == at[:, cut], 1.0, 0.0
            ).astype(jnp.bfloat16)
            for p in range(2):
                hot_s[t, p] = jnp.where(
                    lax.broadcasted_iota(jnp.int32, (2 * n_src, TILE), 0)
                    == src_at[:, cut] + p * n_src, 1.0, 0.0
                ).astype(jnp.bfloat16)

    def table(i, carry):
        at = pl.ds(pl.multiple_of(i * FINE, FINE), FINE)
        for f in range(chunks):
            cut = pl.ds(f * BINS, BINS)
            c1, s1 = coarse_ref[0, pl.ds(i, 1), cut], coarse_ref[1, pl.ds(i, 1), cut]
            c2, s2 = fine_ref[0, :, cut], fine_ref[1, :, cut]
            place = pl.ds(f % PAIRS * BINS, BINS)
            tab[f // PAIRS, 0, at, place] = (c1 * c2 - s1 * s2).astype(jnp.bfloat16)
            tab[f // PAIRS, 1, at, place] = (s1 * c2 + c1 * s2).astype(jnp.bfloat16)
        return carry

    def gather(f):
        wait_halo(f)
        for t in range(tiles):
            rec[t, f] = dot(rows[f], hot_r[t]).astype(jnp.bfloat16)

    def wait_halo(f):
        halo_left(f).wait_recv()
        halo_right(f).wait_recv()

    hots()
    lax.fori_loop(0, coarse_ref.shape[1], table, 0)
    acc[...] = jnp.zeros_like(acc)
    for r in range(rounds):
        for d in range(1, NX):
            x1(r, d).wait_recv()
        total = pick[r * NX + mx]
        for d in range(1, NX):
            total = total + slab_in[r, d - 1]
        slab[r] = total
        for d in range(1, nz):
            z1(r, d).start()
        feed(paces.pop(0))
    for r in range(rounds):
        for d in range(1, nz):
            z1(r, d).wait_recv()
        total = slab[r, mz]
        for d in range(1, nz):
            total = total + part_in[r, d - 1]
        srcs[r * NX + mx, mz] = total
        for d in range(1, nz):
            z2(r, d).start()
        feed(paces.pop(0))
    for r in range(rounds):
        for d in range(1, nz):
            z2(r, d).wait_recv()
        for d in range(1, NX):
            x2(r, d).start()
        feed(paces.pop(0))
    for f in range(pre):
        gather(f)
        feed(1)

    def cross(f, t, early):
        got = rec[t, f].astype(jnp.float32) if early else dot(rows[f], hot_r[t])
        lhs = srcs[f].reshape(BINS, 2 * n_src)
        sr, si = dot(lhs, hot_s[t, 0]), dot(lhs, hot_s[t, 1])
        rr, ri = got[:BINS], got[BINS:]
        real, imag = sr * rr + si * ri, si * rr - sr * ri
        return real.astype(jnp.bfloat16), imag.astype(jnp.bfloat16)

    def wait_sources(r):
        for d in range(1, NX):
            x2(r, d).wait_recv()

    def pair_sum(i, t, early):
        vals = [cross(i * PAIRS + k, t, early) for k in range(PAIRS)]
        return [
            acc[t, p] + dot(tab[i, p], jnp.concatenate([v[p] for v in vals], axis=0))
            for p in range(2)
        ]

    def pair_step(early):
        def run(i, carry):
            if not early:
                for k in range(PAIRS):
                    wait_halo(i * PAIRS + k)
            for t in range(tiles):
                acc[t, 0], acc[t, 1] = pair_sum(i, t, early)
            return carry
        return run

    for r in range(rounds):
        if r * NX // PAIRS < pairs - 1:
            wait_sources(r)
        for early in (True, False):
            low, high = r * NX // PAIRS, min((r + 1) * NX // PAIRS, pairs - 1)
            if early:
                high = min(high, pre // PAIRS)
            else:
                low = max(low, pre // PAIRS)
            if low < high:
                for i in range(low, high):
                    pair_step(early)(i, 0)
                    feed(1)
    feed(chunks)
    if (rounds - 1) * NX // PAIRS >= pairs - 1:
        wait_sources(rounds - 1)
    for k in range(PAIRS):
        wait_halo((pairs - 1) * PAIRS + k)

    def to_core(t):
        return remote(core_out.at[t], core_in.at[t], core_send.at[t], core_recv.at[t], seg=other)

    up, down, far = y_peer(1), y_peer(ny - 1), (my + 2) % ny
    part = out_rows // 2

    def to_relay(t, side):
        return remote(
            relay_out.at[t, side], relay_in.at[t, side],
            relay_send.at[t, side], relay_recv.at[t, side], seg=(up, down)[side],
        )

    def to_y(t, side):
        return remote(
            y_out.at[t, side], y_in.at[t, side],
            y_send.at[t, side], y_recv.at[t, side], seg=(up, down)[side],
        )

    def lag_block(t, j, parity):
        block = j * CORES + parity
        if j >= ny // 2:
            at = pl.ds(pl.multiple_of(block * out_rows - half, out_rows), out_rows)
            return acc[t, 0, at] - acc[t, 1, at]
        at = pl.ds(pl.multiple_of(half - (block + 1) * out_rows, out_rows), out_rows + 8)
        return (acc[t, 0, at] + acc[t, 1, at])[1:out_rows + 1]

    def finish_tile(t):
        acc[t, 0], acc[t, 1] = pair_sum(pairs - 1, t, False)
        for j in range(ny):
            core_out[t, j] = lag_block(t, j, 1 - mc).astype(jnp.bfloat16)
        to_core(t).start()

    def pass_on(t):
        to_core(t).wait_recv()
        for j in range(ny):
            y_own[t, j] = lag_block(t, j, mc) + core_in[t, j].astype(jnp.float32)
        for side in range(2):
            relay_out[t, side] = y_own[t, far, side * part:(side + 1) * part].astype(jnp.bfloat16)
            to_relay(t, side).start()

    def merge(t):
        for side, j in enumerate(((my + 1) % ny, (my + ny - 1) % ny)):
            to_relay(t, side).wait_recv()
            rest = (1 - side) * part
            y_out[t, side, side * part:(side + 1) * part] = (
                y_own[t, j, side * part:(side + 1) * part]
                + relay_in[t, side].astype(jnp.float32)
            ).astype(jnp.bfloat16)
            y_out[t, side, rest:rest + part] = y_own[t, j, rest:rest + part].astype(jnp.bfloat16)
            to_y(t, side).start()

    for t in range(tiles + 2):
        if t < tiles:
            finish_tile(t)
        if 1 <= t <= tiles:
            pass_on(t - 1)
        if t >= 2:
            merge(t - 2)

    place = lax.broadcasted_iota(jnp.int32, (out_rows, out_rows), 0)
    place = jnp.where(my >= ny // 2, place, out_rows - 1 - place)
    order = jnp.where(
        lax.broadcasted_iota(jnp.int32, (out_rows, out_rows), 1) == place, 1.0, 0.0
    ).astype(jnp.bfloat16)
    for t in range(tiles):
        val = y_own[t, my]
        for side in range(2):
            to_y(t, side).wait_recv()
            val = val + y_in[t, side].astype(jnp.float32)
        high = val.astype(jnp.bfloat16)
        rest = val - high.astype(jnp.float32)
        mid = rest.astype(jnp.bfloat16)
        low = (rest - mid.astype(jnp.float32)).astype(jnp.bfloat16)
        out_ref[:, t * TILE:(t + 1) * TILE] = dot(order, high) + (dot(order, mid) + dot(order, low))

    for f in range(max(0, chunks - AHEAD), chunks):
        sent_halo(f)
    for r in range(rounds):
        for d in range(1, NX):
            x1(r, d).wait_send()
            x2(r, d).wait_send()
        for d in range(1, nz):
            z1(r, d).wait_send()
            z2(r, d).wait_send()
    for t in range(tiles):
        to_core(t).wait_send()
        for side in range(2):
            to_relay(t, side).wait_send()
            to_y(t, side).wait_send()


def solution(mesh):
    ny = mesh.shape["seg"] // CORES
    nz = mesh.shape["chan"] // NX

    def per_device(coarse, fine, spectra, source_ids, pair_source, pair_offset, pair_counts):
        _, chans, _, freq = spectra.shape
        chunks = freq // BINS
        slots, n_src = pair_source.shape[0], source_ids.shape[0]
        out_rows = LAGS // (ny * CORES)
        tiles = slots // TILE
        rounds = chunks // NX
        part = (BINS // nz, 2 * n_src)
        taus = coarse.shape[1] * FINE
        bf16, f32, dma = jnp.bfloat16, jnp.float32, pltpu.SemaphoreType.DMA
        vmem = pl.BlockSpec(memory_space=pltpu.VMEM)
        return pl.pallas_call(
            functools.partial(kernel, nz, ny),
            out_shape=jax.ShapeDtypeStruct((out_rows, slots), f32),
            in_specs=[vmem] * 4 + [pl.BlockSpec(memory_space=pl.ANY)] + [vmem] * 2,
            out_specs=vmem,
            scratch_shapes=[
                pltpu.VMEM((chans, 2, freq), bf16),
                pltpu.VMEM((chunks // PAIRS, 2, taus, PAIRS * BINS), bf16),
                pltpu.VMEM((chunks, 2 * BINS, 2 * chans), bf16),
                pltpu.VMEM((chunks, nz, *part), bf16),
                pltpu.VMEM((rounds, NX - 1, nz, *part), bf16),
                pltpu.VMEM((rounds, nz, *part), bf16),
                pltpu.VMEM((rounds, nz - 1, *part), bf16),
                pltpu.VMEM((chunks, nz, *part), bf16),
                pltpu.VMEM((tiles, 2 * chans, TILE), bf16),
                pltpu.VMEM((tiles, 2, 2 * n_src, TILE), bf16),
                pltpu.VMEM((tiles, PRE, 2 * BINS, TILE), bf16),
                pltpu.VMEM((tiles, 2, taus, TILE), f32),
                pltpu.VMEM((tiles, ny, out_rows, TILE), bf16),
                pltpu.VMEM((tiles, ny, out_rows, TILE), bf16),
                pltpu.VMEM((tiles, 2, out_rows // 2, TILE), bf16),
                pltpu.VMEM((tiles, 2, out_rows // 2, TILE), bf16),
                pltpu.VMEM((tiles, 2, out_rows, TILE), bf16),
                pltpu.VMEM((tiles, 2, out_rows, TILE), bf16),
                pltpu.VMEM((tiles, ny, out_rows, TILE), f32),
                dma((chunks,)),
                dma((2, chunks)), dma((2, chunks)),
                dma((rounds, NX - 1)), dma((rounds, NX - 1)),
                dma((rounds, nz - 1)), dma((rounds, nz - 1)),
                dma((rounds, nz - 1)), dma((rounds, nz - 1)),
                dma((rounds, NX - 1)), dma((rounds, NX - 1)),
                dma((tiles,)), dma((tiles,)),
                dma((tiles, 2)), dma((tiles, 2)),
                dma((tiles, 2)), dma((tiles, 2)),
            ],
            compiler_params=pltpu.CompilerParams(
                collective_id=0, has_side_effects=True, vmem_limit_bytes=58 << 20
            ),
            name="correlate",
        )(
            source_ids.reshape(1, n_src), pair_source.reshape(1, slots),
            pair_offset.reshape(1, slots), pair_counts.reshape(1, 1), spectra[0], coarse, fine,
        )

    def call(spectra, source_ids, pair_source, pair_offset, pair_counts):
        coarse, fine = trig_parts(LAGS, spectra.shape[3], spectra.shape[0])
        return jax.shard_map(
            per_device, mesh=mesh,
            in_specs=(
                P(), P(), P("seg", "chan", None, None), P(), P("chan"), P("chan"), P("chan")
            ),
            out_specs=P("seg", "chan"), check_vma=False,
        )(
            jnp.asarray(coarse), jnp.asarray(fine),
            spectra, source_ids, pair_source, pair_offset, pair_counts,
        )

    return call
```

```python
import functools
import math

import jax
import jax.numpy as jnp
import numpy as np
from jax import lax
from jax.experimental import pallas as pl
from jax.experimental.pallas import tpu as pltpu
from jax.sharding import PartitionSpec as P

MESH = pl.DeviceIdType.MESH
LAGS = 1024
WBLOCK = 64
BINS = 256
TILE = 256
CORES = 2
NX = 4
FINE = 16
PAIRS = 2
PRE = 2
PACE = (1, 1, 0, 1, 0, 0, 0)
AHEAD = 2


def trig_parts(lags, freq, segs):
    scale = 1.0 / math.sqrt(freq * segs)
    coarse = lags // 2 // FINE + 1
    bins = np.arange(freq, dtype=np.int64)[None, :]

    def both(tau, factor):
        theta = np.mod(tau[:, None] * bins, 2 * freq) * (math.pi / freq)
        return np.stack([np.cos(theta) * factor, np.sin(theta) * factor]).astype(np.float32)

    return both(np.arange(coarse) * FINE, scale), both(np.arange(FINE), 1.0)


def dot(a, b):
    return jnp.dot(a, b, preferred_element_type=jnp.float32)


def kernel(
    nz, ny, ids_ref, psrc_ref, poff_ref, cnt_ref, raw_hbm, coarse_ref, fine_ref, out_ref,
    raw, tab, rows, pick, slab_in, slab, part_in, srcs, hot_r, hot_s, rec, acc,
    core_out, core_in, relay_out, relay_in, y_out, y_in, y_own,
    raw_sem, halo_send, halo_recv, x1_send, x1_recv, z1_send, z1_recv,
    z2_send, z2_recv, x2_send, x2_recv, core_send, core_recv, relay_send, relay_recv, y_send, y_recv,
):
    chans = raw.shape[0]
    chunks = rows.shape[0]
    band = chans // 2
    slots = psrc_ref.shape[1]
    n_src = ids_ref.shape[1]
    tiles = slots // TILE
    out_rows = out_ref.shape[0]
    half = out_rows * ny
    part_rows = pick.shape[2]
    rounds = chunks // NX
    pairs = chunks // PAIRS
    pre = min(PRE, chunks - PAIRS)
    seg, chan = lax.axis_index("seg"), lax.axis_index("chan")
    n_chan = NX * nz
    my, mc = seg // CORES, seg % CORES
    mz, mx = chan // NX, chan % NX
    left, right = (chan + n_chan - 1) % n_chan, (chan + 1) % n_chan
    other = my * CORES + (1 - mc)

    def x_peer(d):
        return mz * NX + (mx + d) % NX

    def z_peer(d):
        return ((mz + d) % nz) * NX + mx

    def y_peer(d):
        return ((my + d) % ny) * CORES + mc

    def remote(src, dst, send, recv, **where):
        return pltpu.make_async_remote_copy(
            src_ref=src, dst_ref=dst, send_sem=send, recv_sem=recv,
            device_id=where, device_id_type=MESH,
        )

    def read(f):
        cut = pl.ds(pl.multiple_of(f * BINS, BINS), BINS)
        return pltpu.make_async_copy(raw_hbm.at[:, :, cut], raw.at[:, :, cut], raw_sem.at[f])

    for f in range(chunks):
        read(f).start()

    barrier = pltpu.get_barrier_semaphore()
    met = 0
    for peer in [left, right] + [x_peer(d) for d in range(1, NX)] + [z_peer(d) for d in range(1, nz)]:
        pl.semaphore_signal(barrier, inc=1, device_id={"chan": peer}, device_id_type=MESH)
        met += 1
    for peer in [other] + [y_peer(d) for d in range(1, ny)]:
        pl.semaphore_signal(barrier, inc=1, device_id={"seg": peer}, device_id_type=MESH)
        met += 1

    def halo_left(f):
        return remote(
            rows.at[f, :, pl.ds(band, band)], rows.at[f, :, pl.ds(band + chans, band)],
            halo_send.at[0, f], halo_recv.at[0, f], chan=left,
        )

    def halo_right(f):
        return remote(
            rows.at[f, :, pl.ds(2 * band, band)], rows.at[f, :, pl.ds(0, band)],
            halo_send.at[1, f], halo_recv.at[1, f], chan=right,
        )

    local = ids_ref[...] - chan * chans
    inside = (local >= 0) & (local < chans)
    local = jnp.concatenate(
        [jnp.where(inside, local, -1), jnp.where(inside, local + chans, -1)], axis=1
    )
    chosen = jnp.where(
        lax.broadcasted_iota(jnp.int32, (2 * chans, 2 * n_src), 0) == local, 1.0, 0.0
    ).astype(jnp.bfloat16)

    def whiten(f, carry):
        read(f).wait()
        cut = pl.ds(pl.multiple_of(f * BINS, BINS), BINS)
        re, im = [jnp.transpose(raw[:, p, cut].astype(jnp.float32)) for p in range(2)]
        power = re * re + im * im
        level = jnp.mean(power.reshape(BINS // WBLOCK, WBLOCK, chans), axis=1, keepdims=True)
        inverse = jnp.broadcast_to(
            lax.rsqrt(level + 1e-06), (BINS // WBLOCK, WBLOCK, chans)
        ).reshape(BINS, chans)
        white = [(val * inverse).astype(jnp.bfloat16) for val in (re, im)]
        for p in range(2):
            rows[f, pl.ds(p * BINS, BINS), pl.ds(band, chans)] = white[p]
        got = dot(jnp.concatenate(white, axis=1), chosen).astype(jnp.bfloat16)
        for b in range(nz):
            pick[f, b] = got[b * part_rows:(b + 1) * part_rows]
        return carry

    def x1(r, d):
        return remote(
            pick.at[r * NX + (mx + d) % NX], slab_in.at[r, d - 1],
            x1_send.at[r, d - 1], x1_recv.at[r, d - 1], chan=x_peer(d),
        )

    def z1(r, d):
        return remote(
            slab.at[r, (mz + d) % nz], part_in.at[r, d - 1],
            z1_send.at[r, d - 1], z1_recv.at[r, d - 1], chan=z_peer(d),
        )

    def z2(r, d):
        return remote(
            srcs.at[r * NX + mx, mz], srcs.at[r * NX + mx, mz],
            z2_send.at[r, d - 1], z2_recv.at[r, d - 1], chan=z_peer(d),
        )

    def x2(r, d):
        return remote(
            srcs.at[r * NX + mx], srcs.at[r * NX + mx],
            x2_send.at[r, d - 1], x2_recv.at[r, d - 1], chan=x_peer(d),
        )

    for r in range(rounds):
        lax.fori_loop(r * NX, (r + 1) * NX, whiten, 0)
        if r == 0:
            pl.semaphore_wait(barrier, met)
        for d in range(1, NX):
            x1(r, d).start()

    fed = [0]

    def feed(count):
        for _ in range(count):
            f = fed[0]
            if f == chunks:
                return
            if f >= AHEAD:
                sent_halo(f - AHEAD)
            halo_left(f).start()
            halo_right(f).start()
            fed[0] += 1

    def sent_halo(f):
        halo_left(f).wait_send()
        halo_right(f).wait_send()

    paces = list(PACE)
    feed(paces.pop(0))

    def hots():
        at = poff_ref[...] + band
        live = lax.broadcasted_iota(jnp.int32, (1, slots), 1) < cnt_ref[...]
        src_at = jnp.where(live, psrc_ref[...], -4 * n_src)
        for t in range(tiles):
            cut = slice(t * TILE, (t + 1) * TILE)
            hot_r[t] = jnp.where(
                lax.broadcasted_iota(jnp.int32, (2 * chans, TILE), 0) == at[:, cut], 1.0, 0.0
            ).astype(jnp.bfloat16)
            for p in range(2):
                hot_s[t, p] = jnp.where(
                    lax.broadcasted_iota(jnp.int32, (2 * n_src, TILE), 0)
                    == src_at[:, cut] + p * n_src, 1.0, 0.0
                ).astype(jnp.bfloat16)

    def table(i, carry):
        at = pl.ds(pl.multiple_of(i * FINE, FINE), FINE)
        for f in range(chunks):
            cut = pl.ds(f * BINS, BINS)
            c1, s1 = coarse_ref[0, pl.ds(i, 1), cut], coarse_ref[1, pl.ds(i, 1), cut]
            c2, s2 = fine_ref[0, :, cut], fine_ref[1, :, cut]
            place = pl.ds(f % PAIRS * BINS, BINS)
            tab[f // PAIRS, 0, at, place] = (c1 * c2 - s1 * s2).astype(jnp.bfloat16)
            tab[f // PAIRS, 1, at, place] = (s1 * c2 + c1 * s2).astype(jnp.bfloat16)
        return carry

    def gather(f):
        wait_halo(f)
        for t in range(tiles):
            rec[t, f] = dot(rows[f], hot_r[t]).astype(jnp.bfloat16)

    def wait_halo(f):
        halo_left(f).wait_recv()
        halo_right(f).wait_recv()

    hots()
    lax.fori_loop(0, coarse_ref.shape[1], table, 0)
    acc[...] = jnp.zeros_like(acc)
    for r in range(rounds):
        for d in range(1, NX):
            x1(r, d).wait_recv()
        total = pick[r * NX + mx]
        for d in range(1, NX):
            total = total + slab_in[r, d - 1]
        slab[r] = total
        for d in range(1, nz):
            z1(r, d).start()
        feed(paces.pop(0))
    for r in range(rounds):
        for d in range(1, nz):
            z1(r, d).wait_recv()
        total = slab[r, mz]
        for d in range(1, nz):
            total = total + part_in[r, d - 1]
        srcs[r * NX + mx, mz] = total
        for d in range(1, nz):
            z2(r, d).start()
        feed(paces.pop(0))
    for r in range(rounds):
        for d in range(1, nz):
            z2(r, d).wait_recv()
        for d in range(1, NX):
            x2(r, d).start()
        feed(paces.pop(0))
    for f in range(pre):
        gather(f)
        feed(1)

    def cross(f, t, early):
        got = rec[t, f].astype(jnp.float32) if early else dot(rows[f], hot_r[t])
        lhs = srcs[f].reshape(BINS, 2 * n_src)
        sr, si = dot(lhs, hot_s[t, 0]), dot(lhs, hot_s[t, 1])
        rr, ri = got[:BINS], got[BINS:]
        real, imag = sr * rr + si * ri, si * rr - sr * ri
        return real.astype(jnp.bfloat16), imag.astype(jnp.bfloat16)

    def wait_sources(r):
        for d in range(1, NX):
            x2(r, d).wait_recv()

    def pair_sum(i, t, early):
        vals = [cross(i * PAIRS + k, t, early) for k in range(PAIRS)]
        return [
            acc[t, p] + dot(tab[i, p], jnp.concatenate([v[p] for v in vals], axis=0))
            for p in range(2)
        ]

    def pair_step(early):
        def run(i, carry):
            if not early:
                for k in range(PAIRS):
                    wait_halo(i * PAIRS + k)
            for t in range(tiles):
                acc[t, 0], acc[t, 1] = pair_sum(i, t, early)
            return carry
        return run

    for r in range(rounds):
        if r * NX // PAIRS < pairs - 1:
            wait_sources(r)
        for early in (True, False):
            low, high = r * NX // PAIRS, min((r + 1) * NX // PAIRS, pairs - 1)
            if early:
                high = min(high, pre // PAIRS)
            else:
                low = max(low, pre // PAIRS)
            if low < high:
                for i in range(low, high):
                    pair_step(early)(i, 0)
                    feed(1)
    feed(chunks)
    if (rounds - 1) * NX // PAIRS >= pairs - 1:
        wait_sources(rounds - 1)
    for k in range(PAIRS):
        wait_halo((pairs - 1) * PAIRS + k)

    def to_core(t):
        return remote(core_out.at[t], core_in.at[t], core_send.at[t], core_recv.at[t], seg=other)

    up, down, far = y_peer(1), y_peer(ny - 1), (my + 2) % ny
    part = out_rows // 2

    def to_relay(t, side):
        return remote(
            relay_out.at[t, side], relay_in.at[t, side],
            relay_send.at[t, side], relay_recv.at[t, side], seg=(up, down)[side],
        )

    def to_y(t, side):
        return remote(
            y_out.at[t, side], y_in.at[t, side],
            y_send.at[t, side], y_recv.at[t, side], seg=(up, down)[side],
        )

    def lag_block(t, j, parity):
        block = j * CORES + parity
        if j >= ny // 2:
            at = pl.ds(pl.multiple_of(block * out_rows - half, out_rows), out_rows)
            return acc[t, 0, at] - acc[t, 1, at]
        at = pl.ds(pl.multiple_of(half - (block + 1) * out_rows, out_rows), out_rows + 8)
        return (acc[t, 0, at] + acc[t, 1, at])[1:out_rows + 1]

    def finish_tile(t):
        acc[t, 0], acc[t, 1] = pair_sum(pairs - 1, t, False)
        for j in range(ny):
            core_out[t, j] = lag_block(t, j, 1 - mc).astype(jnp.bfloat16)
        to_core(t).start()

    def pass_on(t):
        to_core(t).wait_recv()
        for j in range(ny):
            y_own[t, j] = lag_block(t, j, mc) + core_in[t, j].astype(jnp.float32)
        for side in range(2):
            relay_out[t, side] = y_own[t, far, side * part:(side + 1) * part].astype(jnp.bfloat16)
            to_relay(t, side).start()

    def merge(t):
        for side, j in enumerate(((my + 1) % ny, (my + ny - 1) % ny)):
            to_relay(t, side).wait_recv()
            rest = (1 - side) * part
            y_out[t, side, side * part:(side + 1) * part] = (
                y_own[t, j, side * part:(side + 1) * part]
                + relay_in[t, side].astype(jnp.float32)
            ).astype(jnp.bfloat16)
            y_out[t, side, rest:rest + part] = y_own[t, j, rest:rest + part].astype(jnp.bfloat16)
            to_y(t, side).start()

    for t in range(tiles + 2):
        if t < tiles:
            finish_tile(t)
        if 1 <= t <= tiles:
            pass_on(t - 1)
        if t >= 2:
            merge(t - 2)

    place = lax.broadcasted_iota(jnp.int32, (out_rows, out_rows), 0)
    place = jnp.where(my >= ny // 2, place, out_rows - 1 - place)
    order = jnp.where(
        lax.broadcasted_iota(jnp.int32, (out_rows, out_rows), 1) == place, 1.0, 0.0
    ).astype(jnp.bfloat16)
    for t in range(tiles):
        val = y_own[t, my]
        for side in range(2):
            to_y(t, side).wait_recv()
            val = val + y_in[t, side].astype(jnp.float32)
        high = val.astype(jnp.bfloat16)
        rest = val - high.astype(jnp.float32)
        mid = rest.astype(jnp.bfloat16)
        low = (rest - mid.astype(jnp.float32)).astype(jnp.bfloat16)
        out_ref[:, t * TILE:(t + 1) * TILE] = dot(order, high) + (dot(order, mid) + dot(order, low))

    for f in range(max(0, chunks - AHEAD), chunks):
        sent_halo(f)
    for r in range(rounds):
        for d in range(1, NX):
            x1(r, d).wait_send()
            x2(r, d).wait_send()
        for d in range(1, nz):
            z1(r, d).wait_send()
            z2(r, d).wait_send()
    for t in range(tiles):
        to_core(t).wait_send()
        for side in range(2):
            to_relay(t, side).wait_send()
            to_y(t, side).wait_send()


def solution(mesh):
    ny = mesh.shape["seg"] // CORES
    nz = mesh.shape["chan"] // NX

    def per_device(coarse, fine, spectra, source_ids, pair_source, pair_offset, pair_counts):
        _, chans, _, freq = spectra.shape
        chunks = freq // BINS
        slots, n_src = pair_source.shape[0], source_ids.shape[0]
        out_rows = LAGS // (ny * CORES)
        tiles = slots // TILE
        rounds = chunks // NX
        part = (BINS // nz, 2 * n_src)
        taus = coarse.shape[1] * FINE
        bf16, f32, dma = jnp.bfloat16, jnp.float32, pltpu.SemaphoreType.DMA
        vmem = pl.BlockSpec(memory_space=pltpu.VMEM)
        return pl.pallas_call(
            functools.partial(kernel, nz, ny),
            out_shape=jax.ShapeDtypeStruct((out_rows, slots), f32),
            in_specs=[vmem] * 4 + [pl.BlockSpec(memory_space=pl.ANY)] + [vmem] * 2,
            out_specs=vmem,
            scratch_shapes=[
                pltpu.VMEM((chans, 2, freq), bf16),
                pltpu.VMEM((chunks // PAIRS, 2, taus, PAIRS * BINS), bf16),
                pltpu.VMEM((chunks, 2 * BINS, 2 * chans), bf16),
                pltpu.VMEM((chunks, nz, *part), bf16),
                pltpu.VMEM((rounds, NX - 1, nz, *part), bf16),
                pltpu.VMEM((rounds, nz, *part), bf16),
                pltpu.VMEM((rounds, nz - 1, *part), bf16),
                pltpu.VMEM((chunks, nz, *part), bf16),
                pltpu.VMEM((tiles, 2 * chans, TILE), bf16),
                pltpu.VMEM((tiles, 2, 2 * n_src, TILE), bf16),
                pltpu.VMEM((tiles, PRE, 2 * BINS, TILE), bf16),
                pltpu.VMEM((tiles, 2, taus, TILE), f32),
                pltpu.VMEM((tiles, ny, out_rows, TILE), bf16),
                pltpu.VMEM((tiles, ny, out_rows, TILE), bf16),
                pltpu.VMEM((tiles, 2, out_rows // 2, TILE), bf16),
                pltpu.VMEM((tiles, 2, out_rows // 2, TILE), bf16),
                pltpu.VMEM((tiles, 2, out_rows, TILE), bf16),
                pltpu.VMEM((tiles, 2, out_rows, TILE), bf16),
                pltpu.VMEM((tiles, ny, out_rows, TILE), f32),
                dma((chunks,)),
                dma((2, chunks)), dma((2, chunks)),
                dma((rounds, NX - 1)), dma((rounds, NX - 1)),
                dma((rounds, nz - 1)), dma((rounds, nz - 1)),
                dma((rounds, nz - 1)), dma((rounds, nz - 1)),
                dma((rounds, NX - 1)), dma((rounds, NX - 1)),
                dma((tiles,)), dma((tiles,)),
                dma((tiles, 2)), dma((tiles, 2)),
                dma((tiles, 2)), dma((tiles, 2)),
            ],
            compiler_params=pltpu.CompilerParams(
                collective_id=0, has_side_effects=True, vmem_limit_bytes=58 << 20
            ),
            name="correlate",
        )(
            source_ids.reshape(1, n_src), pair_source.reshape(1, slots),
            pair_offset.reshape(1, slots), pair_counts.reshape(1, 1), spectra[0], coarse, fine,
        )

    def call(spectra, source_ids, pair_source, pair_offset, pair_counts):
        coarse, fine = trig_parts(LAGS, spectra.shape[3], spectra.shape[0])
        return jax.shard_map(
            per_device, mesh=mesh,
            in_specs=(
                P(), P(), P("seg", "chan", None, None), P(), P("chan"), P("chan"), P("chan")
            ),
            out_specs=P("seg", "chan"), check_vma=False,
        )(
            jnp.asarray(coarse), jnp.asarray(fine),
            spectra, source_ids, pair_source, pair_offset, pair_counts,
        )

    return call
```
